128 devices in a mesh: grp: 4 (over x_hi, core), dev: 32 (over x_lo, z, y).
Axes of the slice: x: 4 (x_hi: 2, x_lo: 2; x = x_hi * 2 + x_lo), y: 4, z: 4, core: 2. Of those that a mesh axis runs over, the one named last changes fastest.
Arguments:
- points: float32 [131072, 128], P(('grp', 'dev')), may hold values from -0.6 to 0.6
- weights: float32 [131072, 128], P(('grp', 'dev')), may hold values from -0.12 to 0.12
- skel_index: int32 [128, 128], P(('grp', 'dev')), may hold values from 0 to 1023
- projection: float32 [128, 128, 1024], P(('grp', 'dev')), may hold values from -0.1875 to 0.1875
- top_index: int32 [4, 256], P('grp'), may hold values from 0 to 4095
- subtree_projection: float32 [4, 256, 4096], P('grp', None, 'dev'), may hold values from -0.09375 to 0.09375
- near_leaf_mask: int32 [128, 3], P(('grp', 'dev')), may hold values from 0 to 1, as said below
Outputs:
- potential: float32 [131072, 128], P(('grp', 'dev'))
The draws below stay inside these ranges and needn't reach their ends.
Inputs may be any that keep to these rules, and one draw needn't show every extreme that they name: `near_leaf_mask`: entry [l, 1] (the leaf itself) is 1; entries that name a leaf outside the subtree are 0.
All inputs are finite; a program needn't handle non-finite values.
Results may differ from the reference program's by a relative error of at most 0.0003.
Values sent between devices are 32-bit elements; how exact they have to be, the bound alone decides.
No kernel may reach another device: no remote copies, remote signals or barrier semaphores. Data moves between devices by JAX's collectives and lax.ppermute only.
A program may use at most 64 MiB of HBM per device.

```python
import jax
import jax.numpy as jnp
from jax import lax

D = 128
R = 128
LEAF = 1024
SKEL = 128
SKEL_TOP = 256
LEAF_DEV = 1
GROUPS = 4
LEAVES = 128
POINTS = 131072
CANDS = 4096
N_GRP = 4
N_DEV = 32


def draw_near_leaf_mask(key, part):
    first, second = jax.random.split(jax.random.fold_in(key, 7))
    devices = N_GRP * N_DEV
    slots = 3 * LEAF_DEV
    level = jax.random.randint(first, (devices,), 1, 9)
    noise = jax.random.randint(second, (devices, LEAF_DEV, slots), 0, 8)
    live = (noise < level[:, None, None]).astype(jnp.int32)
    slot_ids = jnp.arange(slots, dtype=jnp.int32)[None, None, :]
    target = jnp.arange(LEAF_DEV, dtype=jnp.int32)[None, :, None]
    position = (jnp.arange(devices, dtype=jnp.int32) % N_DEV)[:, None, None]
    outside = (position == 0) & (slot_ids < LEAF_DEV) | (position == N_DEV - 1) & (slot_ids >= 2 * LEAF_DEV)
    live = jnp.where(outside, 0, live)
    live = jnp.where(slot_ids == LEAF_DEV + target, 1, live)
    return live.reshape(devices * LEAF_DEV, slots)


def touch_ends(values, rng, low, largest):
    place = [jax.random.randint(jax.random.fold_in(rng, axis), (), 0, length) for axis, length in enumerate(values.shape)]
    main_axis = values.shape.index(max(values.shape))
    next_to = place[:main_axis] + [(place[main_axis] + 1) % values.shape[main_axis]] + place[main_axis + 1:]
    return values.at[tuple(place)].set(low).at[tuple(next_to)].set(largest)


def block_levels(own_key, extent, cuts, least, largest):
    gain = 1.0
    for dim, parts in cuts:
        steps = jax.random.uniform(jax.random.fold_in(jax.random.fold_in(own_key, 6), dim), (parts,), jnp.float32, least / len(cuts), largest / len(cuts))
        gain = gain * jnp.repeat(jnp.exp(steps), extent[dim] // parts).reshape((-1,) + (1,) * (len(extent) - 1 - dim))
    return gain


def normal_values(own_key, extent, deviation, reach, shards=(), kind=jnp.bfloat16):
    values = jax.random.normal(own_key, extent, jnp.float32) * deviation
    if len(shards) > 0:
        values = block_levels(own_key, extent, shards, -0.22, 0.18) * values
    return jnp.clip(values, min=-reach, max=reach).astype(kind)


def setup_inputs(seed: int = 0) -> dict:
    key_of = jax.random.split(jax.random.key(seed), 8)
    points = normal_values(key_of[0], (POINTS, D), 0.1, 0.6, ((0, 128),), jnp.float32)
    weights = normal_values(key_of[1], (POINTS, R), 0.02, 0.12, ((0, 128),), jnp.float32)
    skel_index = touch_ends(jax.random.randint(key_of[2], (LEAVES, SKEL), 0, LEAF), jax.random.fold_in(key_of[2], 1), 0, LEAF - 1).astype(jnp.int32)
    projection = normal_values(key_of[3], (LEAVES, SKEL, LEAF), LEAF ** -0.5, 0.1875, ((0, 128),), jnp.float32)
    top_index = touch_ends(jax.random.randint(key_of[4], (GROUPS, SKEL_TOP), 0, CANDS), jax.random.fold_in(key_of[4], 1), 0, CANDS - 1).astype(jnp.int32)
    subtree_projection = normal_values(key_of[5], (GROUPS, SKEL_TOP, CANDS), CANDS ** -0.5, 0.09375, ((0, 4), (2, 32)), jnp.float32)
    near_leaf_mask = draw_near_leaf_mask(jax.random.fold_in(key_of[7], 71), 0)
    return dict(points=points, weights=weights, skel_index=skel_index, projection=projection, top_index=top_index, subtree_projection=subtree_projection, near_leaf_mask=near_leaf_mask)


PRECISION_HIGH = lax.Precision.HIGHEST


def kernel_tile(left, right):
    left_sq = jnp.sum(left * left, axis=1)
    right_sq = jnp.sum(right * right, axis=1)
    cross = jnp.dot(left, right.T, precision=PRECISION_HIGH, preferred_element_type=jnp.float32)
    return jnp.exp(-0.5 * (left_sq[:, None] + right_sq[None, :] - 2.0 * cross))


def pick_rows(table, index):
    return table[index]


def reference(points, weights, skel_index, projection, top_index, subtree_projection, near_leaf_mask):
    leaves = points.shape[0] // LEAF
    per_group = LEAF_DEV * N_DEV
    groups = leaves // per_group
    slots = 3 * LEAF_DEV
    leaf_pts = points.reshape(leaves, LEAF, D)
    leaf_weight_values = weights.reshape(leaves, LEAF, R)
    skeleton_point_rows = jax.vmap(pick_rows)(leaf_pts, skel_index)
    skeleton_weight_values = jnp.einsum("vct,vta->vca", projection, leaf_weight_values, precision=PRECISION_HIGH)
    cand_pts = skeleton_point_rows.reshape(groups, per_group * SKEL, D)
    cand_wts = skeleton_weight_values.reshape(groups, per_group * SKEL, R)
    top_pts = jax.vmap(pick_rows)(cand_pts, top_index).reshape(groups * SKEL_TOP, D)
    top_wts = jnp.einsum("gtc,gcr->gtr", subtree_projection, cand_wts, precision=PRECISION_HIGH).reshape(groups * SKEL_TOP, R)
    top_group = jnp.arange(groups * SKEL_TOP, dtype=jnp.int32) // SKEL_TOP
    cand_leaf = jnp.arange(per_group * SKEL, dtype=jnp.int32) // SKEL
    slot_ids = jnp.arange(slots, dtype=jnp.int32)

    def one_leaf(leaf):
        group = leaf // per_group
        inner = leaf % per_group
        base = (inner // LEAF_DEV - 1) * LEAF_DEV
        target = leaf_pts[leaf]
        mask = near_leaf_mask[leaf].astype(jnp.float32)
        total = jnp.zeros((LEAF, R), jnp.float32)
        for slot in range(slots):
            source = group * per_group + jnp.clip(base + slot, 0, per_group - 1)
            term = jnp.dot(kernel_tile(target, leaf_pts[source]), leaf_weight_values[source], precision=PRECISION_HIGH, preferred_element_type=jnp.float32)
            total = total + mask[slot] * term
        hits = (cand_leaf[:, None] == base + slot_ids[None, :]).astype(jnp.float32)
        near_col = jnp.sum(hits * mask[None, :], axis=1)
        far_w = cand_wts[group] * (1.0 - near_col)[:, None]
        total = total + jnp.dot(kernel_tile(target, cand_pts[group]), far_w, precision=PRECISION_HIGH, preferred_element_type=jnp.float32)
        top_w = top_wts * (top_group != group).astype(jnp.float32)[:, None]
        total = total + jnp.dot(kernel_tile(target, top_pts), top_w, precision=PRECISION_HIGH, preferred_element_type=jnp.float32)
        return total

    result = lax.map(one_leaf, jnp.arange(leaves, dtype=jnp.int32))
    return result.reshape(leaves * LEAF, R)
```

```python
import functools
import math

import jax
import jax.numpy as jnp
from jax import lax
from jax.experimental import pallas as pl
from jax.experimental.pallas import tpu as pltpu
from jax.sharding import PartitionSpec as P


LOG2E = math.log2(math.e)
BF = jnp.bfloat16
F32 = jnp.float32
VMEM = pl.BlockSpec(memory_space=pltpu.VMEM)
SMEM = pl.BlockSpec(memory_space=pltpu.SMEM)
NX, NZ, NY = 2, 4, 4
ROWS = 256


def halves(x):
    hi = x.astype(BF)
    return hi, (x - hi.astype(F32)).astype(BF)


def thirds(x):
    hi = x.astype(BF)
    rest = x - hi.astype(F32)
    mid = rest.astype(BF)
    return hi, mid, (rest - mid.astype(F32)).astype(BF)


def dot_nt(a, b):
    return lax.dot_general(a, b, (((1,), (1,)), ((), ())), preferred_element_type=F32)


def dot_nn(a, b):
    return lax.dot_general(a, b, (((1,), (0,)), ((), ())), preferred_element_type=F32)


def dot_tn(a, b):
    return lax.dot_general(a, b, (((0,), (0,)), ((), ())), preferred_element_type=F32)


def dot_full(a, b):
    ah, al = halves(a)
    bh, bl = halves(b)
    return dot_nn(ah, bh) + (dot_nn(ah, bl) + dot_nn(al, bh))


def prep_kernel(skel_ref, near_ref, top_ref, pts_ref, wts_ref, proj_ref, sub_ref, block_ref, mine_ref, other_ref, joined_ref, picked, part, sems):
    feats = pts_ref.shape[1]
    skel = block_ref.shape[0]
    half = mine_ref.shape[0]
    copies = [
        pltpu.make_async_copy(ref, joined_ref.at[:, pl.ds(c * feats, feats)], sems.at[c])
        for c, ref in enumerate((pts_ref, wts_ref))
    ]
    for c in copies:
        c.start()

    def pick(i, carry):
        picked[pl.ds(i, 1), :] = pts_ref[pl.ds(skel_ref[0, i], 1), :]
        return carry

    lax.fori_loop(0, skel, pick, 0, unroll=16)
    block_ref[:, :feats] = picked[...]
    block_ref[:, feats:] = dot_full(proj_ref[0], wts_ref[...])
    pos = lax.axis_index("dev")
    rows = lax.broadcasted_iota(jnp.int32, (skel, top_ref.shape[1]), 0) + pos * skel
    hot = (rows == top_ref[...]).astype(F32).astype(BF)
    hi, mid, lo = thirds(picked[...])
    part[:, :feats] = dot_tn(hot, hi) + (dot_tn(hot, mid) + dot_tn(hot, lo))
    part[:, feats:] = dot_full(sub_ref[0], block_ref[:, feats:])
    x = pos // (NZ * NY)
    mine_ref[...] = part[pl.ds(pl.multiple_of(x * half, half), half), :]
    other_ref[:half, :] = part[pl.ds(pl.multiple_of((1 - x) * half, half), half), :]
    for slot in range(8):
        value = near_ref[0, min(slot, 2)].astype(F32)
        other_ref[half + slot:half + slot + 1, :] = jnp.full((1, 2 * feats), value, F32)
    for c in copies:
        c.wait()


def prepare(near, skel_index, top_index, points, weights, projection, subtree_projection):
    skel = skel_index.shape[1]
    feats = points.shape[1]
    half = top_index.shape[1] // NX
    return pl.pallas_call(
        prep_kernel,
        out_shape=(
            jax.ShapeDtypeStruct((skel, 2 * feats), F32),
            jax.ShapeDtypeStruct((half, 2 * feats), F32),
            jax.ShapeDtypeStruct((half + 8, 2 * feats), F32),
            jax.ShapeDtypeStruct((points.shape[0], 2 * feats), F32),
        ),
        in_specs=[SMEM] * 2 + [VMEM] * 5,
        out_specs=(VMEM, VMEM, VMEM, pl.BlockSpec(memory_space=pl.ANY)),
        scratch_shapes=[pltpu.VMEM((skel, feats), F32), pltpu.VMEM((NX * half, 2 * feats), F32), pltpu.SemaphoreType.DMA((2,))],
        name="prep",
    )(skel_index, near, top_index, points, weights, projection, subtree_projection)


WIDTH = {"pair": 2, "pick": 3}


class Chosen:
    def __init__(self, copies, choice):
        self.copies, self.choice = copies, choice

    def start(self):
        for n, copy in enumerate(self.copies):
            pl.when(self.choice == n)(copy.start)

    def wait(self):
        self.copies[0].wait()


def tiles_kernel(chunks, first, last, across, near_hbm, tgt_hbm, *refs):
    count = sum(WIDTH.get(kind[0], 1) for chunk in chunks for kind, _ in chunk)
    if not first:
        total_hbm, refs = refs[0], refs[1:]
    src_hbm, refs = refs[:count], refs[count:]
    out_ref, near, tgt, cat, total, sems = refs[:6]
    bufs = refs[6:]
    leaf, feats = tgt.shape
    tail = near_hbm.shape[0] - near.shape[0]
    copies = [
        pltpu.make_async_copy(near_hbm.at[pl.ds(tail, 8), pl.ds(0, feats)], near, sems.at[0]),
        pltpu.make_async_copy(tgt_hbm, tgt, sems.at[1]),
    ]
    pos = lax.axis_index("dev")
    waits, i = [], 0
    for chunk, buf in zip(chunks, bufs):
        mine, row = [], 0
        for kind, shape in chunk:
            rows = pl.ds(row, shape[0])
            if kind[0] == "pair":
                for c in range(2):
                    part = buf.at[rows, pl.ds(c * feats, feats)]
                    mine.append(pltpu.make_async_copy(src_hbm[i + c], part, sems.at[2 + i + c]))
                i += 2
            elif kind[0] == "pick":
                if kind[1] == 0:
                    choice = jnp.where(pos == NZ * NY, 2, jnp.where((pos % NY == 0) & (pos > 0), 1, 0))
                else:
                    choice = jnp.where(pos == NZ * NY - 1, 2, jnp.where((pos % NY == NY - 1) & (pos < NX * NZ * NY - 1), 1, 0))
                each = [pltpu.make_async_copy(src_hbm[i + c], buf.at[rows, :], sems.at[2 + i]) for c in range(3)]
                mine.append(Chosen(each, choice))
                i += 3
            else:
                mine.append(pltpu.make_async_copy(src_hbm[i], buf.at[rows, :], sems.at[2 + i]))
                i += 1
            row += shape[0]
        copies += mine
        waits.append(mine)
    if not first:
        copies.append(pltpu.make_async_copy(total_hbm, total, sems.at[2 + count]))
    for c in copies:
        c.start()
    copies[0].wait()
    copies[1].wait()
    hi, lo = halves(tgt[...] * LOG2E)
    cat[:, :feats] = hi
    cat[:, feats:] = lo
    own = (pos + NZ * NY) % (NX * NZ * NY) if across else pos
    x, z, y = pos // (NZ * NY), (pos // NY) % NZ, pos % NY

    def far_keep(k, j):
        leaf_id = device(x, z + (NZ - k), y + (0, 3, 1, 2)[j])
        keep = jnp.ones((1, feats), F32)
        for slot in range(3):
            hit = (leaf_id - own + 1 == slot).astype(F32)
            keep = keep - hit * near[slot:slot + 1, :]
        return keep

    for n, (chunk, buf) in enumerate(zip(chunks, bufs)):
        for c in waits[n]:
            c.wait()
        src = buf[:, :feats]
        parts, row = [], 0
        for kind, shape in chunk:
            if kind[0] == "far":
                each = shape[0] // NY
                for j in range(NY):
                    parts.append(buf[row + j * each:row + (j + 1) * each, feats:] * far_keep(kind[1], j))
            elif kind[0] == "top":
                parts.append(buf[row:row + shape[0], feats:])
            else:
                parts.append(buf[row:row + shape[0], feats:] * near[kind[1]:kind[1] + 1, :])
            row += shape[0]
        wts = parts[0] if len(parts) == 1 else jnp.concatenate(parts, axis=0)
        wts = wts * jnp.exp(-0.5 * jnp.sum(src * src, axis=1, keepdims=True))
        src_hi, src_lo = halves(src)
        src_twice = jnp.concatenate([src_hi, src_hi], axis=1)
        w_cat = jnp.concatenate(halves(wts), axis=1)
        if n == 0 and not first:
            copies[-1].wait()
        for m in range(0, leaf, ROWS):
            at = pl.ds(m, ROWS)
            arg = dot_nt(cat[at, :], src_twice) + dot_nt(cat[at, :feats], src_lo)
            e_hi, e_lo = halves(jnp.exp2(arg))
            both = dot_nn(e_hi, w_cat) + dot_nn(e_lo, w_cat)
            value = both[:, :feats] + both[:, feats:]
            if not (first and n == 0):
                value = value + total[at, :]
            if n < len(chunks) - 1:
                total[at, :] = value
            else:
                if last:
                    here = tgt[at, :]
                    value = value * jnp.exp(-0.5 * jnp.sum(here * here, axis=1, keepdims=True))
                out_ref[at, :] = value


def add_tiles(across, near, targets, chunks, total=None, last=False):
    leaf, feats = targets.shape
    first = total is None
    arrays = [a for chunk in chunks for _, *group in chunk for a in group]
    shapes = [[(kind, group[0].shape) for kind, *group in chunk] for chunk in chunks]
    args = [near, targets] + ([] if first else [total]) + arrays
    sizes = [sum(shape[0] for _, shape in chunk) for chunk in shapes]
    rows = sum(sizes)
    return pl.pallas_call(
        functools.partial(tiles_kernel, shapes, first, last, across),
        out_shape=jax.ShapeDtypeStruct((leaf, feats), F32),
        in_specs=[pl.BlockSpec(memory_space=pl.ANY)] * len(args),
        out_specs=VMEM,
        scratch_shapes=[
            pltpu.VMEM((8, feats), F32),
            pltpu.VMEM((leaf, feats), F32),
            pltpu.VMEM((leaf, 2 * feats), BF),
            pltpu.VMEM((leaf, feats), F32),
            pltpu.SemaphoreType.DMA((len(arrays) + 3,)),
        ]
        + [pltpu.VMEM((size, 2 * feats), F32) for size in sizes],
        compiler_params=pltpu.CompilerParams(vmem_limit_bytes=40 << 20),
        cost_estimate=pl.CostEstimate(
            flops=16 * leaf * rows * feats, transcendentals=leaf * rows, bytes_accessed=8 * (rows + 2 * leaf) * feats
        ),
        name="tiles",
    )(*args)


def place(i):
    return i // (NZ * NY), (i // NY) % NZ, i % NY


def device(x, z, y):
    return (x % NX) * NZ * NY + (z % NZ) * NY + y % NY


def shift(a, dx, dz, dy):
    pairs = []
    for i in range(NX * NZ * NY):
        x, z, y = place(i)
        pairs.append((i, device(x + dx, z + dz, y + dy)))
    return lax.ppermute(a, "dev", pairs)


def swap(a, bz, by):
    pairs = []
    for i in range(NX * NZ * NY):
        x, z, y = place(i)
        pairs.append((i, device(x, z ^ bz, y ^ by)))
    return lax.ppermute(a, "dev", pairs)


def group_swap(a, bit):
    return lax.ppermute(a, "grp", [(i, i ^ bit) for i in range(4)])


def local(points, weights, skel_index, projection, top_index, subtree_projection, near_leaf_mask):
    targets = shift(points, 1, 0, 0)
    block, mine, other, joined = prepare(
        near_leaf_mask, skel_index, top_index, points, weights, projection, subtree_projection
    )
    own_near = other

    ring = (1, 3, 2)
    by_y = [block]
    for k in ring:
        by_y.append(shift(block, 0, 0, k))
    plane = jnp.concatenate(by_y, axis=0)
    by_z = {0: plane}
    for k in ring:
        by_z[k] = shift(plane, 0, k, 0)

    count = lax.axis_size("dev")
    count = lax.axis_size("dev")
    middle = NZ * NY
    inside = [i for i in range(1, count) if i % NY]
    above = [lax.ppermute(joined, "dev", [(i - 1, i) for i in inside])]
    below = [lax.ppermute(joined, "dev", [(i, i - 1) for i in inside])]
    for ends in ([i for i in range(NY, count, NY) if i != middle], [middle]):
        pairs = [(i - 1, i) for i in ends] + [(i, i - 1) for i in ends]
        corner = lax.ppermute(joined, "dev", pairs)
        above.append(corner)
        below.append(corner)

    got = shift(other, 1, 0, 0)
    mine = mine + got[: mine.shape[0]]
    for bz, by in ((1, 0), (3, 0), (0, 1), (0, 3)):
        peer = swap(mine, bz, by)
        mine = mine + peer
    two = group_swap(mine, 1)
    pair_of = jnp.concatenate([mine, two], axis=0)
    four = group_swap(pair_of, 2)

    far = lambda k: (("far", k), by_z[k])
    top = [(("top",), two), (("top",), four)]
    total = add_tiles(False, own_near, points, [[(("pair", 1), points, weights)]])
    side = add_tiles(True, got, targets, [[far(0)]])
    side = add_tiles(True, got, targets, [[far(1), far(3)]], side)
    side = add_tiles(True, got, targets, [[far(2)] + top], side, last=True)
    back = shift(side, 1, 0, 0)
    total = add_tiles(False, own_near, points, [[far(0), far(2)] + top, [far(1), far(3)]], total)
    total = add_tiles(False, own_near, points, [[(("pick", 0), *above)], [(("pick", 2), *below)]], total, last=True)
    return total + back


def solution(mesh):
    return jax.shard_map(
        local,
        mesh=mesh,
        in_specs=(
            P(("grp", "dev"), None),
            P(("grp", "dev"), None),
            P(("grp", "dev"), None),
            P(("grp", "dev"), None, None),
            P("grp", None),
            P("grp", None, "dev"),
            P(("grp", "dev"), None),
        ),
        out_specs=P(("grp", "dev"), None),
        check_vma=False,
    )
```

```python
import functools
import math

import jax
import jax.numpy as jnp
from jax import lax
from jax.experimental import pallas as pl
from jax.experimental.pallas import tpu as pltpu
from jax.sharding import PartitionSpec as P


LOG2E = math.log2(math.e)
BF = jnp.bfloat16
F32 = jnp.float32
VMEM = pl.BlockSpec(memory_space=pltpu.VMEM)
SMEM = pl.BlockSpec(memory_space=pltpu.SMEM)
NX, NZ, NY = 2, 4, 4
ROWS = 256


def halves(x):
    hi = x.astype(BF)
    return hi, (x - hi.astype(F32)).astype(BF)


def thirds(x):
    hi = x.astype(BF)
    rest = x - hi.astype(F32)
    mid = rest.astype(BF)
    return hi, mid, (rest - mid.astype(F32)).astype(BF)


def dot_nt(a, b):
    return lax.dot_general(a, b, (((1,), (1,)), ((), ())), preferred_element_type=F32)


def dot_nn(a, b):
    return lax.dot_general(a, b, (((1,), (0,)), ((), ())), preferred_element_type=F32)


def dot_tn(a, b):
    return lax.dot_general(a, b, (((0,), (0,)), ((), ())), preferred_element_type=F32)


def dot_full(a, b):
    ah, al = halves(a)
    bh, bl = halves(b)
    return dot_nn(ah, bh) + (dot_nn(ah, bl) + dot_nn(al, bh))


def prep_kernel(skel_ref, near_ref, top_ref, pts_ref, wts_ref, proj_ref, sub_ref, block_ref, mine_ref, other_ref, joined_ref, picked, part, sems):
    feats = pts_ref.shape[1]
    skel = block_ref.shape[0]
    half = mine_ref.shape[0]
    copies = [
        pltpu.make_async_copy(ref, joined_ref.at[:, pl.ds(c * feats, feats)], sems.at[c])
        for c, ref in enumerate((pts_ref, wts_ref))
    ]
    for c in copies:
        c.start()

    def pick(i, carry):
        picked[pl.ds(i, 1), :] = pts_ref[pl.ds(skel_ref[0, i], 1), :]
        return carry

    lax.fori_loop(0, skel, pick, 0, unroll=16)
    block_ref[:, :feats] = picked[...]
    block_ref[:, feats:] = dot_full(proj_ref[0], wts_ref[...])
    pos = lax.axis_index("dev")
    rows = lax.broadcasted_iota(jnp.int32, (skel, top_ref.shape[1]), 0) + pos * skel
    hot = (rows == top_ref[...]).astype(F32).astype(BF)
    hi, mid, lo = thirds(picked[...])
    part[:, :feats] = dot_tn(hot, hi) + (dot_tn(hot, mid) + dot_tn(hot, lo))
    part[:, feats:] = dot_full(sub_ref[0], block_ref[:, feats:])
    x = pos // (NZ * NY)
    mine_ref[...] = part[pl.ds(pl.multiple_of(x * half, half), half), :]
    other_ref[:half, :] = part[pl.ds(pl.multiple_of((1 - x) * half, half), half), :]
    for slot in range(8):
        value = near_ref[0, min(slot, 2)].astype(F32)
        other_ref[half + slot:half + slot + 1, :] = jnp.full((1, 2 * feats), value, F32)
    for c in copies:
        c.wait()


def prepare(near, skel_index, top_index, points, weights, projection, subtree_projection):
    skel = skel_index.shape[1]
    feats = points.shape[1]
    half = top_index.shape[1] // NX
    return pl.pallas_call(
        prep_kernel,
        out_shape=(
            jax.ShapeDtypeStruct((skel, 2 * feats), F32),
            jax.ShapeDtypeStruct((half, 2 * feats), F32),
            jax.ShapeDtypeStruct((half + 8, 2 * feats), F32),
            jax.ShapeDtypeStruct((points.shape[0], 2 * feats), F32),
        ),
        in_specs=[SMEM] * 2 + [VMEM] * 5,
        out_specs=(VMEM, VMEM, VMEM, pl.BlockSpec(memory_space=pl.ANY)),
        scratch_shapes=[pltpu.VMEM((skel, feats), F32), pltpu.VMEM((NX * half, 2 * feats), F32), pltpu.SemaphoreType.DMA((2,))],
        name="prep",
    )(skel_index, near, top_index, points, weights, projection, subtree_projection)


WIDTH = {"pair": 2, "inner": 2, "outer": 4}


class Chosen:
    def __init__(self, lists, choice):
        self.lists, self.choice = lists, choice

    def start(self):
        for n, copies in enumerate(self.lists):
            @pl.when(self.choice == n)
            def _(copies=copies):
                for copy in copies:
                    copy.start()

    def wait(self):
        self.lists[0][0].wait()


def tiles_kernel(chunks, first, last, across, final, near_hbm, tgt_hbm, *refs):
    count = sum(WIDTH.get(kind[0], 1) for chunk in chunks for kind, _ in chunk)
    if not first:
        total_hbm, refs = refs[0], refs[1:]
    src_hbm, refs = refs[:count], refs[count:]
    if final:
        back_hbm, refs = refs[0], refs[1:]
    out_ref, near, tgt, cat, total, sems = refs[:6]
    bufs = refs[6:]
    if final:
        back, bufs = bufs[-1], bufs[:-1]
    leaf, feats = tgt.shape
    tail = near_hbm.shape[0] - near.shape[0]
    copies = [
        pltpu.make_async_copy(near_hbm.at[pl.ds(tail, 8), pl.ds(0, feats)], near, sems.at[0]),
        pltpu.make_async_copy(tgt_hbm, tgt, sems.at[1]),
    ]
    pos = lax.axis_index("dev")
    waits, i = [], 0
    for chunk, buf in zip(chunks, bufs):
        mine, row = [], 0
        for kind, shape in chunk:
            rows = pl.ds(row, shape[0])
            if kind[0] == "pair":
                for c in range(2):
                    part = buf.at[rows, pl.ds(c * feats, feats)]
                    mine.append(pltpu.make_async_copy(src_hbm[i + c], part, sems.at[2 + i + c]))
                i += 2
            elif kind[0] in ("inner", "outer"):
                whole = [
                    [pltpu.make_async_copy(src_hbm[i + c], buf.at[rows, :], sems.at[2 + i])] for c in range(2)
                ]
                if kind[0] == "inner":
                    mine.append(Chosen(whole, (pos % NY == 0).astype(jnp.int32)))
                else:
                    both = [
                        pltpu.make_async_copy(src_hbm[i + 2 + c], buf.at[rows, pl.ds(c * feats, feats)], sems.at[2 + i])
                        for c in range(2)
                    ]
                    corner = (pos % NY == 0) | (pos % NY == NY - 1)
                    middle = (pos == NZ * NY) | (pos == NZ * NY - 1)
                    mine.append(Chosen(whole + [both], jnp.where(middle, 2, jnp.where(corner, 1, 0))))
                i += WIDTH[kind[0]]
            else:
                mine.append(pltpu.make_async_copy(src_hbm[i], buf.at[rows, :], sems.at[2 + i]))
                i += 1
            row += shape[0]
        copies += mine
        waits.append(mine)
    if not first:
        copies.append(pltpu.make_async_copy(total_hbm, total, sems.at[2 + count]))
    for c in copies:
        c.start()
    if final:
        back_copy = pltpu.make_async_copy(back_hbm, back, sems.at[3 + count])
        back_copy.start()
    copies[0].wait()
    copies[1].wait()
    hi, lo = halves(tgt[...] * LOG2E)
    cat[:, :feats] = hi
    cat[:, feats:] = lo
    own = (pos + NZ * NY) % (NX * NZ * NY) if across else pos
    x, z, y = pos // (NZ * NY), (pos // NY) % NZ, pos % NY

    def far_keep(k, j):
        leaf_id = device(x, z + (NZ - k), y + (0, 3, 1, 2)[j])
        keep = jnp.ones((1, feats), F32)
        for slot in range(3):
            hit = (leaf_id - own + 1 == slot).astype(F32)
            keep = keep - hit * near[slot:slot + 1, :]
        return keep

    for n, (chunk, buf) in enumerate(zip(chunks, bufs)):
        for c in waits[n]:
            c.wait()
        src = buf[:, :feats]
        parts, row = [], 0
        for kind, shape in chunk:
            if kind[0] == "far":
                each = shape[0] // NY
                for j in range(NY):
                    parts.append(buf[row + j * each:row + (j + 1) * each, feats:] * far_keep(kind[1], j))
            elif kind[0] in ("inner", "outer"):
                low = (pos % NY == 0) == (kind[0] == "outer")
                keep = jnp.where(low, near[0:1, :], near[2:3, :])
                parts.append(buf[row:row + shape[0], feats:] * keep)
            elif kind[0] == "top":
                parts.append(buf[row:row + shape[0], feats:])
            else:
                parts.append(buf[row:row + shape[0], feats:] * near[kind[1]:kind[1] + 1, :])
            row += shape[0]
        wts = parts[0] if len(parts) == 1 else jnp.concatenate(parts, axis=0)
        wts = wts * jnp.exp(-0.5 * jnp.sum(src * src, axis=1, keepdims=True))
        src_hi, src_lo = halves(src)
        src_twice = jnp.concatenate([src_hi, src_hi], axis=1)
        w_cat = jnp.concatenate(halves(wts), axis=1)
        if n == 0 and not first:
            copies[-1].wait()
        if n == len(chunks) - 1 and final:
            back_copy.wait()
        for m in range(0, leaf, ROWS):
            at = pl.ds(m, ROWS)
            arg = dot_nt(cat[at, :], src_twice) + dot_nt(cat[at, :feats], src_lo)
            e_hi, e_lo = halves(jnp.exp2(arg))
            both = dot_nn(e_hi, w_cat) + dot_nn(e_lo, w_cat)
            value = both[:, :feats] + both[:, feats:]
            if not (first and n == 0):
                value = value + total[at, :]
            if n < len(chunks) - 1:
                total[at, :] = value
            else:
                if last:
                    here = tgt[at, :]
                    value = value * jnp.exp(-0.5 * jnp.sum(here * here, axis=1, keepdims=True))
                if final:
                    value = value + back[at, :]
                out_ref[at, :] = value


def add_tiles(across, near, targets, chunks, total=None, last=False, back=None):
    leaf, feats = targets.shape
    first = total is None
    arrays = [a for chunk in chunks for _, *group in chunk for a in group]
    shapes = [[(kind, group[0].shape) for kind, *group in chunk] for chunk in chunks]
    args = [near, targets] + ([] if first else [total]) + arrays + ([] if back is None else [back])
    sizes = [sum(shape[0] for _, shape in chunk) for chunk in shapes]
    rows = sum(sizes)
    return pl.pallas_call(
        functools.partial(tiles_kernel, shapes, first, last, across, back is not None),
        out_shape=jax.ShapeDtypeStruct((leaf, feats), F32),
        in_specs=[pl.BlockSpec(memory_space=pl.ANY)] * len(args),
        out_specs=VMEM,
        scratch_shapes=[
            pltpu.VMEM((8, feats), F32),
            pltpu.VMEM((leaf, feats), F32),
            pltpu.VMEM((leaf, 2 * feats), BF),
            pltpu.VMEM((leaf, feats), F32),
            pltpu.SemaphoreType.DMA((len(arrays) + 4,)),
        ]
        + [pltpu.VMEM((size, 2 * feats), F32) for size in sizes]
        + ([] if back is None else [pltpu.VMEM((leaf, feats), F32)]),
        compiler_params=pltpu.CompilerParams(vmem_limit_bytes=40 << 20),
        cost_estimate=pl.CostEstimate(
            flops=16 * leaf * rows * feats, transcendentals=leaf * rows, bytes_accessed=8 * (rows + 2 * leaf) * feats
        ),
        name="tiles",
    )(*args)


def place(i):
    return i // (NZ * NY), (i // NY) % NZ, i % NY


def device(x, z, y):
    return (x % NX) * NZ * NY + (z % NZ) * NY + y % NY


def shift(a, dx, dz, dy):
    pairs = []
    for i in range(NX * NZ * NY):
        x, z, y = place(i)
        pairs.append((i, device(x + dx, z + dz, y + dy)))
    return lax.ppermute(a, "dev", pairs)


def swap(a, bz, by):
    pairs = []
    for i in range(NX * NZ * NY):
        x, z, y = place(i)
        pairs.append((i, device(x, z ^ bz, y ^ by)))
    return lax.ppermute(a, "dev", pairs)


def group_swap(a, bit):
    return lax.ppermute(a, "grp", [(i, i ^ bit) for i in range(4)])


def local(points, weights, skel_index, projection, top_index, subtree_projection, near_leaf_mask):
    targets = shift(points, 1, 0, 0)
    block, mine, other, joined = prepare(
        near_leaf_mask, skel_index, top_index, points, weights, projection, subtree_projection
    )
    own_near = other

    ring = (1, 3, 2)
    by_y = [block]
    for k in ring:
        by_y.append(shift(block, 0, 0, k))
    plane = jnp.concatenate(by_y, axis=0)
    by_z = {0: plane}
    for k in ring:
        by_z[k] = shift(plane, 0, k, 0)

    count = lax.axis_size("dev")
    count = lax.axis_size("dev")
    middle = NZ * NY
    inside = [i for i in range(1, count) if i % NY]
    above = lax.ppermute(joined, "dev", [(i - 1, i) for i in inside])
    below = lax.ppermute(joined, "dev", [(i, i - 1) for i in inside])
    both_ways = lambda ends: [(i - 1, i) for i in ends] + [(i, i - 1) for i in ends]
    corner = lax.ppermute(joined, "dev", both_ways([i for i in range(NY, count, NY) if i != middle]))
    corner_points = lax.ppermute(points, "dev", both_ways([middle]))
    corner_weights = lax.ppermute(weights, "dev", both_ways([middle]))

    got = shift(other, 1, 0, 0)
    mine = mine + got[: mine.shape[0]]
    for bz, by in ((1, 0), (3, 0), (0, 1), (0, 3)):
        peer = swap(mine, bz, by)
        mine = mine + peer
    two = group_swap(mine, 1)
    pair_of = jnp.concatenate([mine, two], axis=0)
    four = group_swap(pair_of, 2)

    far = lambda k: (("far", k), by_z[k])
    top = [(("top",), two), (("top",), four)]
    total = add_tiles(False, own_near, points, [[(("pair", 1), points, weights)]])
    side = add_tiles(True, got, targets, [[far(0)]])
    side = add_tiles(True, got, targets, [[far(1), far(3)]], side)
    side = add_tiles(True, got, targets, [[far(2)] + top], side, last=True)
    back = shift(side, 1, 0, 0)
    inner = (("inner",), above, below)
    outer = (("outer",), below, corner, corner_points, corner_weights)
    total = add_tiles(
        False, own_near, points, [[far(0), far(2)] + top, [far(1), far(3)], [inner]], total
    )
    total = add_tiles(False, own_near, points, [[outer]], total, last=True)
    return total + back


def solution(mesh):
    return jax.shard_map(
        local,
        mesh=mesh,
        in_specs=(
            P(("grp", "dev"), None),
            P(("grp", "dev"), None),
            P(("grp", "dev"), None),
            P(("grp", "dev"), None, None),
            P("grp", None),
            P("grp", None, "dev"),
            P(("grp", "dev"), None),
        ),
        out_specs=P(("grp", "dev"), None),
        check_vma=False,
    )
```
